32 devices in a mesh: seq: 4 (over y, x), hv: 8 (over z, core).
Axes of the slice: x: 2, y: 2, z: 4, core: 2. Of those that a mesh axis runs over, the one named last changes fastest.
Arguments:
- qproj: bfloat16 [8192, 2048], P(('seq', 'hv')), may hold values from -6 to 6
- kproj: bfloat16 [8192, 2048], P(('seq', 'hv')), may hold values from -6 to 6
- vproj: bfloat16 [8192, 4096], P(('seq', 'hv')), may hold values from -40 to 40
- igate: bfloat16 [8192, 8], P(('seq', 'hv')), may hold values from -10 to 10
- fgate: bfloat16 [8192, 8], P(('seq', 'hv')), may hold values from -0.1 to 24
- ogate: bfloat16 [8192, 4096], P(('seq', 'hv')), may hold values from -8 to 8
- norm_gain: bfloat16 [4096], replicated, may hold values from 0.099609375 to 1.8984375
Outputs:
- gated: bfloat16 [8192, 4096], P(('seq', 'hv'))
The draws below stay inside these ranges and needn't reach their ends.
All inputs are finite; a program needn't handle non-finite values.
Results may differ from the reference program's by a relative error of at most 0.0052.
Values may be sent and summed in bfloat16 or wider, within the bound.
No kernel may reach another device: no remote copies, remote signals or barrier semaphores. Data moves between devices by JAX's collectives and lax.ppermute only.
A program may use at most 64 MiB of HBM per device.

```python
import math
import jax
import jax.numpy as jnp
from jax import lax

HEAD_COUNT = 8
DK = 256
DV = 512
TOK_DEV = 256
BLOCK = 512
TOKEN_COUNT = 8192


def draw_fgate(key, part):
    key_ordering, key_dispersion, key_positions, key_sample_group, key_runs = jax.random.split(key, 5)
    nslow = HEAD_COUNT // 2
    order = jax.random.permutation(key_ordering, HEAD_COUNT)
    slow = order < nslow
    run_count = TOKEN_COUNT // TOK_DEV
    fast_runs = jax.random.uniform(key_runs, (run_count, HEAD_COUNT), jnp.float32, 0.0, 1.0) < 0.5
    fast_tokens = jnp.repeat(fast_runs, TOK_DEV, axis=0)
    fast_flag = jnp.logical_and(jnp.logical_not(slow)[None, :], fast_tokens)
    spread = jnp.exp(jax.random.uniform(key_dispersion, (TOKEN_COUNT, HEAD_COUNT), jnp.float32, math.log(0.5), math.log(2.0)))
    speed_factor = jnp.where(fast_flag, 1.0 / 40.0, 0.5 / TOKEN_COUNT) * spread
    spots = jax.random.randint(key_positions, (2, HEAD_COUNT), 0, TOKEN_COUNT)
    places = jnp.arange(TOKEN_COUNT)[:, None]
    matched_flag = (places == spots[0][None, :]) | (places == spots[1][None, :])
    sample_group = jax.random.uniform(key_sample_group, (TOKEN_COUNT, HEAD_COUNT), jnp.float32, 0.22, 0.69)
    speed_factor = jnp.where(matched_flag, sample_group, speed_factor)
    return (-jnp.log(jnp.expm1(speed_factor))).astype(jnp.bfloat16)


def draw_vproj(key, part):
    k_base, k_cols, k_rows = jax.random.split(key, 3)
    width = HEAD_COUNT * DV
    col_scale = jnp.exp(jax.random.uniform(k_cols, (1, width), jnp.float32, math.log(0.3), math.log(3.0)))
    base = jax.random.truncated_normal(k_base, -4.0, 4.0, (TOKEN_COUNT, width), jnp.float32)
    row_scale = jnp.exp(jax.random.uniform(k_rows, (TOKEN_COUNT, 1), jnp.float32, math.log(0.3), math.log(3.0)))
    values = base * col_scale * row_scale
    return values.astype(jnp.bfloat16)


def level_of(stream_key, shape, shards, least, high):
    def one(dim, parts):
        draws = jax.random.uniform(jax.random.fold_in(jax.random.fold_in(stream_key, 6), dim), (parts,), jnp.float32, least / len(shards), high / len(shards))
        return jnp.repeat(jnp.exp(draws), shape[dim] // parts).reshape((-1,) + (1,) * (len(shape) - dim - 1))

    factor_of = one(*shards[0])
    for cut in shards[1:]:
        factor_of = factor_of * one(*cut)
    return factor_of


def gaussian(stream_key, shape, scale, most, cuts=(), held_as=jnp.bfloat16):
    entries = jax.random.normal(stream_key, shape, jnp.float32) * scale
    if len(cuts) > 0:
        entries = level_of(stream_key, shape, cuts, -0.22, 0.18) * entries
    return jnp.clip(entries, min=-most, max=most).astype(held_as)


def setup_inputs(seed: int = 0) -> dict:
    keys = jax.random.split(jax.random.key(seed), 8)
    qproj = gaussian(keys[0], (TOKEN_COUNT, HEAD_COUNT * DK), 1.0, 6.0, ((0, 32),))
    kproj = gaussian(keys[1], (TOKEN_COUNT, HEAD_COUNT * DK), 1.0, 6.0, ((0, 32),))
    vproj = draw_vproj(jax.random.fold_in(keys[7], 71), 0)
    igate = gaussian(keys[3], (TOKEN_COUNT, HEAD_COUNT), 2.0, 10.0, ((0, 32),))
    fgate = draw_fgate(jax.random.fold_in(keys[7], 71), 0)
    ogate = gaussian(keys[5], (TOKEN_COUNT, HEAD_COUNT * DV), 1.5, 8.0, ((0, 32),))
    norm_gain = jnp.clip(1.0 + 0.18 * jax.random.normal(keys[6], (HEAD_COUNT * DV,), jnp.float32), 0.099609375, 1.8984375).astype(jnp.bfloat16)
    return dict(qproj=qproj, kproj=kproj, vproj=vproj, igate=igate, fgate=fgate, ogate=ogate, norm_gain=norm_gain)


def block_step(state, inputs):
    query, key_rows, value_rows, in_gate, fo_gate = inputs
    scale = math.sqrt(DK)
    in_log = 15.0 * jnp.tanh(in_gate.astype(jnp.float32) / 15.0)
    fo_log = jax.nn.log_sigmoid(fo_gate.astype(jnp.float32))
    cumul = jnp.cumsum(fo_log)
    size = query.shape[0]
    rows = lax.broadcasted_iota(jnp.int32, (size, size), 0)
    cols = lax.broadcasted_iota(jnp.int32, (size, size), 1)
    causal = cols <= rows
    log_weight = jnp.where(causal, cumul[:, None] - cumul[None, :] + in_log[None, :], -jnp.inf)
    weight = jnp.exp(log_weight)
    scores = jnp.dot(query, key_rows.T, preferred_element_type=jnp.float32) / scale
    product = scores * weight
    numer = jnp.dot(product.astype(jnp.bfloat16), value_rows, preferred_element_type=jnp.float32)
    query_f = query.astype(jnp.float32)
    decay = jnp.exp(cumul)
    numer = numer + decay[:, None] * jnp.dot(query_f, state, precision=lax.Precision.HIGHEST) / scale
    hval = numer.astype(jnp.bfloat16)
    g_last = cumul[-1]
    w_end = jnp.exp(g_last - cumul + in_log)
    key_w = key_rows.astype(jnp.float32) * w_end[:, None]
    state = jnp.exp(g_last) * state + jnp.dot(key_w.T, value_rows.astype(jnp.float32), precision=lax.Precision.HIGHEST)
    return (state, hval)

def one_head(inputs):
    start = jnp.zeros((DK, DV), jnp.float32)
    final, outputs = lax.scan(block_step, start, inputs)
    return outputs

def reference(qproj, kproj, vproj, igate, fgate, ogate, norm_gain):
    nblocks = TOKEN_COUNT // BLOCK
    q_heads = qproj.reshape(TOKEN_COUNT, HEAD_COUNT, DK).transpose(1, 0, 2).reshape(HEAD_COUNT, nblocks, BLOCK, DK)
    k_heads = kproj.reshape(TOKEN_COUNT, HEAD_COUNT, DK).transpose(1, 0, 2).reshape(HEAD_COUNT, nblocks, BLOCK, DK)
    v_heads = vproj.reshape(TOKEN_COUNT, HEAD_COUNT, DV).transpose(1, 0, 2).reshape(HEAD_COUNT, nblocks, BLOCK, DV)
    i_heads = igate.T.reshape(HEAD_COUNT, nblocks, BLOCK)
    f_heads = fgate.T.reshape(HEAD_COUNT, nblocks, BLOCK)
    hval = lax.map(one_head, (q_heads, k_heads, v_heads, i_heads, f_heads))
    hval = hval.reshape(HEAD_COUNT, TOKEN_COUNT, DV).transpose(1, 0, 2)
    hfloat = hval.astype(jnp.float32)
    meansq = lax.optimization_barrier(jnp.mean(hfloat * hfloat, axis=2, keepdims=True))
    normed = hfloat * lax.rsqrt(meansq + 1e-06)
    gain = norm_gain.astype(jnp.float32).reshape(1, HEAD_COUNT, DV)
    gate = jax.nn.sigmoid(ogate.astype(jnp.float32).reshape(TOKEN_COUNT, HEAD_COUNT, DV))
    return (normed * gain * gate).reshape(TOKEN_COUNT, HEAD_COUNT * DV).astype(jnp.bfloat16)
```

```python
import functools
import math

import jax
import jax.numpy as jnp
from jax import lax
from jax.experimental import pallas as pl
from jax.experimental.pallas import tpu as pltpu
from jax.sharding import Mesh
from jax.sharding import PartitionSpec as P

F32 = jnp.float32
BF16 = jnp.bfloat16
CORES = 2
PAD = 16
CHUNKS = 1


def call(kernel, outs, ins, scal, scratch=(), grid=(), in_specs=None, out_specs=None, aliases=None, name=None):
    whole = lambda a: pl.BlockSpec(a.shape, lambda *_: (0,) * len(a.shape))
    if in_specs is None:
        in_specs = [whole(a) for a in ins]
    if out_specs is None:
        out_specs = [whole(a) for a in outs]
    return pl.pallas_call(
        kernel,
        out_shape=outs,
        grid_spec=pltpu.PrefetchScalarGridSpec(
            num_scalar_prefetch=1,
            grid=grid if grid else (1,),
            in_specs=in_specs,
            out_specs=out_specs,
            scratch_shapes=list(scratch),
        ),
        input_output_aliases=aliases or {},
        compiler_params=pltpu.CompilerParams(dimension_semantics=("arbitrary",)),
        name=name,
    )(scal, *ins)


def shape(dims, dtype):
    return jax.ShapeDtypeStruct(dims, dtype)


def pick(table, head):
    lanes = lax.broadcasted_iota(jnp.int32, table.shape, 1)
    return jnp.sum(jnp.where(lanes == head, table, 0.0), axis=1, keepdims=True)


def gates_kernel(scal, ig, fg, rowa, colg, colw, total):
    heads, tok = ig.shape
    il = 15.0 * jnp.tanh(ig[...].astype(F32) / 15.0)
    lf = jax.nn.log_sigmoid(fg[...].astype(F32))
    earlier = lax.broadcasted_iota(jnp.int32, (tok, tok), 0)
    later = lax.broadcasted_iota(jnp.int32, (tok, tok), 1)
    tri = (earlier <= later).astype(F32)
    g = jnp.dot(lf, tri, precision=lax.Precision.HIGHEST, preferred_element_type=F32)
    last = g[:, tok - 1 : tok]
    rowa[...] = il - g
    both = jnp.concatenate([g, jnp.exp(last - g + il)], axis=0).T
    colg[...] = both[:, :heads]
    colw[...] = both[:, heads:]
    total[...] = jnp.broadcast_to(last, total.shape)


def state_kernel(scal, k, v, colw, own, other, *, first, per, half):
    step = pl.program_id(0)
    mine = step < per
    core = scal[0]
    head = jnp.where(mine, core * half + first + step, (1 - core) * half + first + step - per)
    kw = k[...].astype(F32) * pick(colw[...], head)
    high = kw.astype(BF16)
    low = (kw - high.astype(F32)).astype(BF16)
    dims = (((0,), (0,)), ((), ()))
    value = v[...]
    part = lax.dot_general(high, value, dims, preferred_element_type=F32)
    part = part + lax.dot_general(low, value, dims, preferred_element_type=F32)

    @pl.when(mine)
    def _():
        own[...] = part

    @pl.when(jnp.logical_not(mine))
    def _():
        other[...] = part


def put_log(ref, start, value):
    high = value.astype(BF16).astype(F32)
    mid = (value - high).astype(BF16).astype(F32)
    low = value - high - mid
    rows = lax.broadcasted_iota(jnp.int32, (PAD, value.shape[1]), 0)
    ref[start:, :] = jnp.where(rows == 0, high, jnp.where(rows == 1, mid, low)).astype(BF16)


def get_log(ref, start):
    tile = ref[start:, :].astype(F32)
    return tile[0:1] + tile[1:2] + tile[2:3]


def chip_kernel(scal, own, rec, total, rtotal, *msgs, first, half, dkey, rows):
    core, place = scal[0], scal[1]
    nz = len(msgs)
    zero = core == 0
    for k in range(nz):
        dest = lax.rem(place + k, nz)
        here = pl.ds(pl.multiple_of(dest * rows, rows), rows)
        head = core * half + first + (dest * rows) // dkey
        a, b = own[here, :], rec[here, :]
        ga, gb = total[pl.ds(head, 1), :], rtotal[pl.ds(head, 1), :]
        g1 = jnp.where(zero, gb, ga)
        state = jnp.exp(g1) * jnp.where(zero, a, b) + jnp.where(zero, b, a)
        msgs[k][0:rows, :] = state.astype(BF16)
        put_log(msgs[k], rows, ga + gb)


def column_kernel(scal, *refs, rows):
    msgs, out = refs[:-1], refs[-1]
    nz = len(msgs)
    place = scal[1]
    logs = [get_log(m, rows) for m in msgs]
    places = [lax.rem(place - k + nz, nz) for k in range(nz)]
    total = jnp.zeros((rows, out.shape[1]), F32)
    for k in range(nz):
        after = jnp.zeros_like(logs[0])
        for j in range(nz):
            if j != k:
                after = after + jnp.where(places[j] > places[k], logs[j], 0.0)
        total = total + jnp.exp(after) * msgs[k][0:rows, :].astype(F32)
    out[0:rows, :] = total.astype(BF16)
    put_log(out, rows, functools.reduce(lambda x, y: x + y, logs))


def prefix_kernel(scal, *refs, rows, nz, spans):
    msgs, cols, outs = refs[:nz], refs[nz : nz + spans], refs[nz + spans : 2 * nz + spans]
    states, logs, pres = refs[2 * nz + spans :]
    place = scal[1]
    for k in range(nz):
        source = lax.rem(place - k + nz, nz)
        states[source] = msgs[k][0:rows, :].astype(F32)
        logs[source] = jnp.broadcast_to(get_log(msgs[k], rows), logs.shape[1:])
    state = jnp.zeros(states.shape[1:], F32)
    decay = jnp.zeros((1, states.shape[2]), F32)
    for col in cols:
        state = state + jnp.exp(decay) * col[0:rows, :].astype(F32)
        decay = decay + get_log(col, rows)
    for z in range(nz):
        pres[z] = state.astype(BF16)
        state = jnp.exp(logs[z][0:1, :]) * state + states[z]
    for k in range(nz):
        outs[k][...] = pres[lax.rem(place + k, nz)]


def spread_kernel(scal, *refs, first, half, dkey, rows, nz):
    parts = refs[:nz]
    own, rec, total, rtotal, mine, other = refs[nz:]
    core, place = scal[0], scal[1]
    zero = core == 0
    for k in range(nz):
        source = lax.rem(place - k + nz, nz)
        here = pl.ds(pl.multiple_of(source * rows, rows), rows)
        head = core * half + first + (source * rows) // dkey
        g0 = jnp.where(zero, total[pl.ds(head, 1), :], rtotal[pl.ds(head, 1), :])
        s0 = jnp.where(zero, own[here, :], rec[here, :])
        before = parts[k][...].astype(F32)
        after = jnp.exp(g0) * before + s0
        mine[here, :] = jnp.where(zero, before, after).astype(BF16)
        other[here, :] = jnp.where(zero, after, before).astype(BF16)


def intra_kernel(scal, q, k, v, rowa, colg, out, *, scale):
    head = pl.program_id(0)
    tok = q.shape[0]
    rows = lax.broadcasted_iota(jnp.int32, (tok, tok), 0)
    cols = lax.broadcasted_iota(jnp.int32, (tok, tok), 1)
    scores = lax.dot_general(q[...], k[...], (((1,), (1,)), ((), ())), preferred_element_type=F32) / scale
    logw = jnp.where(cols <= rows, pick(colg[...], head) + rowa[pl.ds(head, 1), :], -jnp.inf)
    prod = (scores * jnp.exp(logw)).astype(BF16)
    out[...] = jnp.dot(prod, v[...], preferred_element_type=F32)


def final_kernel(scal, *refs, first, per, half, scale, aliased):
    q, mine, rec, intra, og, gain, colg = refs[:7]
    out = refs[-1]
    step = pl.program_id(0)
    core = scal[0]
    own = step < per
    head = jnp.where(own, core * half + first + step, (1 - core) * half + first + step - per)
    state = jnp.where(own, mine[...], rec[...])
    inter = jnp.dot(q[...], state, preferred_element_type=F32)
    numer = intra[...] + jnp.exp(pick(colg[...], head)) * inter / scale
    hval = numer.astype(BF16).astype(F32)
    meansq = jnp.mean(hval * hval, axis=1, keepdims=True)
    normed = hval * lax.rsqrt(meansq + 1e-06)
    gate = jax.nn.sigmoid(og[...].astype(F32))
    out[...] = (normed * gain[...].astype(F32) * gate).astype(BF16)


def shards(qproj, kproj, vproj, igate, fgate, ogate, norm_gain):
    spans, nz = lax.axis_size("seq"), lax.axis_size("z")
    tok, heads = igate.shape
    dkey = qproj.shape[1] // heads
    dval = vproj.shape[1] // heads
    half = heads // CORES
    per = half // CHUNKS
    rows = per * dkey // nz
    assert rows % PAD == 0 and dkey % rows == 0
    scale = math.sqrt(dkey)
    scal = jnp.stack([lax.axis_index("core"), lax.axis_index("z")]).astype(jnp.int32)
    swap = [(0, 1), (1, 0)]

    rowa, colg, colw, total = call(
        gates_kernel,
        [shape((heads, tok), F32), shape((tok, heads), F32), shape((tok, heads), F32), shape((heads, dval), F32)],
        [igate.T, fgate.T],
        scal,
        name="gates",
    )
    rtotal = lax.ppermute(total, "core", swap)
    whole = lambda a: pl.BlockSpec(a.shape, lambda *_: (0,) * len(a.shape))

    def head_at(step, s, first):
        return jnp.where(step < per, s[0] * half + first + step, (1 - s[0]) * half + first + step - per)

    chunks = []
    for i in range(CHUNKS):
        first = i * per
        at = lambda j, s, first=first: (0, head_at(j, s, first))
        own, other = call(
            functools.partial(state_kernel, first=first, per=per, half=half),
            [shape((per * dkey, dval), F32)] * 2,
            [kproj, vproj, colw],
            scal,
            grid=(2 * per,),
            in_specs=[pl.BlockSpec((tok, dkey), at), pl.BlockSpec((tok, dval), at), whole(colw)],
            out_specs=[
                pl.BlockSpec((dkey, dval), lambda j, s: (jnp.minimum(j, per - 1), 0)),
                pl.BlockSpec((dkey, dval), lambda j, s: (jnp.maximum(j - per, 0), 0)),
            ],
            name=f"state{i}",
        )
        rec = lax.ppermute(other, "core", swap)
        chunks.append((first, own, rec))

    sent = []
    for i, (first, own, rec) in enumerate(chunks):
        msgs = call(
            functools.partial(chip_kernel, first=first, half=half, dkey=dkey, rows=rows),
            [shape((rows + PAD, dval), BF16)] * nz,
            [own, rec, total, rtotal],
            scal,
            name=f"chip{i}",
        )
        sent.append(
            [msgs[0]]
            + [lax.ppermute(msgs[k], "z", [(j, (j + k) % nz) for j in range(nz)]) for k in range(1, nz)]
        )

    intra = call(
        functools.partial(intra_kernel, scale=scale),
        [shape((tok, heads * dval), F32)],
        [qproj, kproj, vproj, rowa, colg],
        scal,
        grid=(heads,),
        in_specs=[
            pl.BlockSpec((tok, dkey), lambda j, s: (0, j)),
            pl.BlockSpec((tok, dkey), lambda j, s: (0, j)),
            pl.BlockSpec((tok, dval), lambda j, s: (0, j)),
            whole(rowa),
            whole(colg),
        ],
        out_specs=[pl.BlockSpec((tok, dval), lambda j, s: (0, j))],
        name="intra",
    )[0]

    out = None
    gain = norm_gain.reshape(1, heads * dval)
    for i, (first, own, rec) in enumerate(chunks):
        msgs = sent[i]
        column = call(
            functools.partial(column_kernel, rows=rows),
            [shape((rows + PAD, dval), BF16)],
            msgs,
            scal,
            name=f"column{i}",
        )[0]
        cols = [
            lax.ppermute(column, "seq", [(j, j + k) for j in range(spans - k)]) for k in range(1, spans)
        ]
        pres = call(
            functools.partial(prefix_kernel, rows=rows, nz=nz, spans=len(cols)),
            [shape((rows, dval), BF16)] * nz,
            list(msgs) + cols,
            scal,
            scratch=[
                pltpu.VMEM((nz, rows, dval), F32),
                pltpu.VMEM((nz, 8, dval), F32),
                pltpu.VMEM((nz, rows, dval), BF16),
            ],
            name=f"prefix{i}",
        )
        parts = [pres[0]] + [
            lax.ppermute(pres[k], "z", [(j, (j + k) % nz) for j in range(nz)]) for k in range(1, nz)
        ]
        mine, other = call(
            functools.partial(spread_kernel, first=first, half=half, dkey=dkey, rows=rows, nz=nz),
            [shape((per * dkey, dval), BF16)] * 2,
            parts + [own, rec, total, rtotal],
            scal,
            name=f"spread{i}",
        )
        back = lax.ppermute(other, "core", swap)
        at = lambda j, s, first=first: (0, head_at(j, s, first))
        ins = [qproj, mine, back, intra, ogate, gain, colg]
        specs = [
            pl.BlockSpec((tok, dkey), at),
            pl.BlockSpec((dkey, dval), lambda j, s: (jnp.minimum(j, per - 1), 0)),
            pl.BlockSpec((dkey, dval), lambda j, s: (jnp.maximum(j - per, 0), 0)),
            pl.BlockSpec((tok, dval), at),
            pl.BlockSpec((tok, dval), at),
            pl.BlockSpec((1, dval), at),
            whole(colg),
        ]
        aliases = None
        if out is not None:
            ins.append(out)
            specs.append(pl.BlockSpec(memory_space=pl.ANY))
            aliases = {len(ins): 0}
        out = call(
            functools.partial(final_kernel, first=first, per=per, half=half, scale=scale, aliased=out is not None),
            [shape((tok, heads * dval), BF16)],
            ins,
            scal,
            grid=(2 * per,),
            in_specs=specs,
            out_specs=[pl.BlockSpec((tok, dval), at)],
            aliases=aliases,
            name=f"final{i}",
        )[0]
    return out


def solution(mesh):
    spans, lanes = mesh.shape["seq"], mesh.shape["hv"]
    inner = Mesh(mesh.devices.reshape(spans, lanes // CORES, CORES), ("seq", "z", "core"))
    split = P(("seq", "z", "core"), None)
    return jax.shard_map(
        shards, mesh=inner, in_specs=(split,) * 6 + (P(),), out_specs=split, check_vma=False
    )
```

```python
import functools
import math

import jax
import jax.numpy as jnp
from jax import lax
from jax.experimental import pallas as pl
from jax.experimental.pallas import tpu as pltpu
from jax.sharding import Mesh
from jax.sharding import PartitionSpec as P

F32 = jnp.float32
BF16 = jnp.bfloat16
CORES = 2
PAD = 16
CHUNKS = 2


def call(kernel, outs, ins, name, scratch=()):
    vmem = pl.BlockSpec(memory_space=pltpu.VMEM)
    return pl.pallas_call(
        kernel,
        out_shape=outs,
        in_specs=[vmem] * len(ins),
        out_specs=[vmem] * len(outs),
        scratch_shapes=list(scratch),
        compiler_params=pltpu.CompilerParams(vmem_limit_bytes=8 << 20),
        name=name,
    )(*ins)


def shape(dims, dtype):
    return jax.ShapeDtypeStruct(dims, dtype)


def rows_at(start, size):
    return pl.ds(pl.multiple_of(start, size), size)


def head_cols(j, half, width):
    head = lax.rem(lax.axis_index("core") * half + j, CORES * half)
    return pl.ds(pl.multiple_of(head * width, width), width)


def gates_kernel(ig, fg, rowa, cols, total, *, scale):
    heads, tok = ig.shape
    half = heads // CORES
    zero = lax.axis_index("core") == 0
    own_first = lambda a: jnp.where(zero, a, jnp.concatenate([a[half:], a[:half]], axis=0))
    il = own_first(15.0 * jnp.tanh(ig[...].astype(F32) / 15.0))
    lf = own_first(jax.nn.log_sigmoid(fg[...].astype(F32)))
    earlier = lax.broadcasted_iota(jnp.int32, (tok, tok), 0)
    later = lax.broadcasted_iota(jnp.int32, (tok, tok), 1)
    tri = (earlier <= later).astype(F32).astype(BF16)
    high = lf.astype(BF16)
    rest = lf - high.astype(F32)
    mid = rest.astype(BF16)
    low = (rest - mid.astype(F32)).astype(BF16)
    sums = lambda a: jnp.dot(a, tri, preferred_element_type=F32)
    g = sums(high) + sums(mid) + sums(low)
    last = g[:, tok - 1 : tok]
    rowa[...] = il - g
    cols[...] = jnp.concatenate([g, jnp.exp(last - g + il), jnp.exp(g) / scale], axis=0).T
    total[...] = jnp.broadcast_to(last, total.shape)


def state_kernel(k, v, cols, out, *, first, per, half):
    heads = CORES * half
    dkey, dval = out.shape[0] // per, out.shape[1]
    dims = (((0,), (0,)), ((), ()))
    for j in range(per):
        weight = cols[:, heads + first + j : heads + first + j + 1]
        kw = k[:, head_cols(first + j, half, dkey)].astype(F32) * weight
        high = kw.astype(BF16)
        low = (kw - high.astype(F32)).astype(BF16)
        value = v[:, head_cols(first + j, half, dval)]
        part = lax.dot_general(high, value, dims, preferred_element_type=F32)
        out[j * dkey : (j + 1) * dkey, :] = part + lax.dot_general(low, value, dims, preferred_element_type=F32)


def put_log(ref, start, value):
    high = value.astype(BF16).astype(F32)
    mid = (value - high).astype(BF16).astype(F32)
    low = value - high - mid
    rows = lax.broadcasted_iota(jnp.int32, (PAD, value.shape[1]), 0)
    ref[start:, :] = jnp.where(rows == 0, high, jnp.where(rows == 1, mid, low)).astype(BF16)


def get_log(ref, start):
    tile = ref[start:, :].astype(F32)
    return tile[0:1] + tile[1:2] + tile[2:3]


def chip_kernel(own, rec, total, rtotal, *msgs, first, half, dkey, rows):
    place, zero = lax.axis_index("z"), lax.axis_index("core") == 0
    nz = len(msgs)
    for k in range(nz):
        dest = lax.rem(place + k, nz)
        here = rows_at(dest * rows, rows)
        head = first + (dest * rows) // dkey
        ga, gb = total[pl.ds(head, 1), :], rtotal[pl.ds(head + half, 1), :]
        decay = jnp.exp(jnp.where(zero, gb, ga))
        a, b = own[here, :], rec[here, :]
        state = decay * jnp.where(zero, a, b) + jnp.where(zero, b, a)
        msgs[k][0:rows, :] = state.astype(BF16)
        put_log(msgs[k], rows, ga + gb)


def column_kernel(*refs, rows):
    msgs, out = refs[:-1], refs[-1]
    nz = len(msgs)
    place = lax.axis_index("z")
    logs = [get_log(m, rows) for m in msgs]
    places = [lax.rem(place - k + nz, nz) for k in range(nz)]
    total = jnp.zeros((rows, out.shape[1]), F32)
    for k in range(nz):
        after = jnp.zeros_like(logs[0])
        for j in range(nz):
            if j != k:
                after = after + jnp.where(places[j] > places[k], logs[j], 0.0)
        total = total + jnp.exp(after) * msgs[k][0:rows, :].astype(F32)
    out[0:rows, :] = total.astype(BF16)
    put_log(out, rows, functools.reduce(lambda x, y: x + y, logs))


def prefix_kernel(*refs, rows, nz, spans):
    msgs, cols, outs = refs[:nz], refs[nz : nz + spans], refs[nz + spans : 2 * nz + spans]
    states, logs, pres = refs[2 * nz + spans :]
    place = lax.axis_index("z")
    for k in range(nz):
        source = lax.rem(place - k + nz, nz)
        states[source] = msgs[k][0:rows, :].astype(F32)
        logs[source] = jnp.broadcast_to(get_log(msgs[k], rows), logs.shape[1:])
    state = jnp.zeros(states.shape[1:], F32)
    decay = jnp.zeros((1, states.shape[2]), F32)
    for col in cols:
        state = state + jnp.exp(decay) * col[0:rows, :].astype(F32)
        decay = decay + get_log(col, rows)
    for z in range(nz):
        pres[z] = state.astype(BF16)
        state = jnp.exp(logs[z][0:1, :]) * state + states[z]
    for k in range(nz):
        outs[k][...] = pres[lax.rem(place + k, nz)]


def spread_kernel(*refs, first, half, dkey, rows, nz):
    parts = refs[:nz]
    own, rec, total, rtotal, mine, other = refs[nz:]
    place, zero = lax.axis_index("z"), lax.axis_index("core") == 0
    for k in range(nz):
        source = lax.rem(place - k + nz, nz)
        here = rows_at(source * rows, rows)
        head = first + (source * rows) // dkey
        decay = jnp.exp(jnp.where(zero, total[pl.ds(head, 1), :], rtotal[pl.ds(head + half, 1), :]))
        before = parts[k][...].astype(F32)
        after = decay * before + jnp.where(zero, own[here, :], rec[here, :])
        mine[here, :] = jnp.where(zero, before, after).astype(BF16)
        other[here, :] = jnp.where(zero, after, before).astype(BF16)


def intra_kernel(q, k, v, rowa, cols, out, *, half, dkey, dval, scale):
    tok = q.shape[0]
    rows = lax.broadcasted_iota(jnp.int32, (tok, tok), 0)
    lanes = lax.broadcasted_iota(jnp.int32, (tok, tok), 1)
    causal = lanes <= rows
    for j in range(CORES * half):
        at = head_cols(j, half, dkey)
        scores = lax.dot_general(q[:, at], k[:, at], (((1,), (1,)), ((), ())), preferred_element_type=F32)
        logw = jnp.where(causal, cols[:, j : j + 1] + rowa[j : j + 1, :], -jnp.inf)
        prod = (scores / scale * jnp.exp(logw)).astype(BF16)
        out[:, j * dval : (j + 1) * dval] = jnp.dot(
            prod, v[:, head_cols(j, half, dval)], preferred_element_type=F32
        )


def final_kernel(scal, q, state, intra, cols, og, gain, *rest, first, per, half):
    out = rest[-1]
    heads = CORES * half
    dkey, dval = state.shape[0] // per, state.shape[1]
    for j in range(per):
        head = first + j
        here = slice(j * dval, (j + 1) * dval)
        inter = jnp.dot(
            q[:, head_cols(head, half, dkey)], state[j * dkey : (j + 1) * dkey, :], preferred_element_type=F32
        )
        decay = cols[:, 2 * heads + head : 2 * heads + head + 1]
        numer = intra[:, head * dval : (head + 1) * dval] + decay * inter
        hval = numer.astype(BF16).astype(F32)
        meansq = jnp.mean(hval * hval, axis=1, keepdims=True)
        normed = hval * lax.rsqrt(meansq + 1e-06)
        gate = jax.nn.sigmoid(og[:, here].astype(F32))
        out[:, here] = (normed * gain[:, here].astype(F32) * gate).astype(BF16)


def final(scal, q, state, intra, cols, og, gain, out, *, first, per, half, dval, name):
    tok = q.shape[0]
    blocks = CORES * half // per
    at = lambda j, s: (0, lax.rem(s[0] * (half // per) + first // per, blocks))
    vmem = pl.BlockSpec(memory_space=pltpu.VMEM)
    ins = [q, state, intra, cols, og, gain]
    specs = [vmem, vmem, vmem, vmem, pl.BlockSpec((tok, per * dval), at), pl.BlockSpec((1, per * dval), at)]
    aliases = {}
    if out is not None:
        ins.append(out)
        specs.append(pl.BlockSpec(memory_space=pl.ANY))
        aliases = {len(ins): 0}
    return pl.pallas_call(
        functools.partial(final_kernel, first=first, per=per, half=half),
        out_shape=shape((tok, CORES * half * dval), BF16),
        grid_spec=pltpu.PrefetchScalarGridSpec(
            num_scalar_prefetch=1,
            grid=(1,),
            in_specs=specs,
            out_specs=pl.BlockSpec((tok, per * dval), at),
        ),
        input_output_aliases=aliases,
        compiler_params=pltpu.CompilerParams(vmem_limit_bytes=8 << 20),
        name=name,
    )(scal, *ins)


def after(value, *others):
    return lax.optimization_barrier((value,) + others)[0]


def shards(qproj, kproj, vproj, igate, fgate, ogate, norm_gain):
    spans, nz = lax.axis_size("seq"), lax.axis_size("z")
    tok, heads = igate.shape
    dkey = qproj.shape[1] // heads
    dval = vproj.shape[1] // heads
    half = heads // CORES
    per = half // CHUNKS
    rows = per * dkey // nz
    assert rows % PAD == 0 and dkey % rows == 0
    scale = math.sqrt(dkey)
    swap = [(0, 1), (1, 0)]
    turn = lambda a, k: lax.ppermute(a, "z", [(j, (j + k) % nz) for j in range(nz)])

    rowa, cols, total = call(
        functools.partial(gates_kernel, scale=scale),
        [shape((heads, tok), F32), shape((tok, 3 * heads), F32), shape((heads, dval), F32)],
        [igate.T, fgate.T],
        "gates",
    )
    rtotal = lax.ppermute(total, "core", swap)

    def state(first, name):
        return call(
            functools.partial(state_kernel, first=first, per=per, half=half),
            [shape((per * dkey, dval), F32)],
            [kproj, vproj, cols],
            name,
        )[0]

    chunks = []
    for i in range(CHUNKS):
        rec = lax.ppermute(state(half + i * per, f"state_other{i}"), "core", swap)
        own = state(i * per, f"state_own{i}")
        chunks.append((i * per, own, rec))

    sent = []
    for i, (first, own, rec) in enumerate(chunks):
        msgs = call(
            functools.partial(chip_kernel, first=first, half=half, dkey=dkey, rows=rows),
            [shape((rows + PAD, dval), BF16)] * nz,
            [own, rec, total, rtotal],
            f"chip{i}",
        )
        sent.append([msgs[0]] + [turn(msgs[k], k) for k in range(1, nz)])

    intra = call(
        functools.partial(intra_kernel, half=half, dkey=dkey, dval=dval, scale=scale),
        [shape((tok, heads * dval), F32)],
        [qproj, kproj, vproj, rowa, after(cols, sent[-1][0])],
        "intra",
    )[0]
    sent[0][0] = after(sent[0][0], intra)

    scal = lax.axis_index("core").astype(jnp.int32).reshape(1)
    gain = norm_gain.reshape(1, heads * dval)
    columns = []
    for i in range(CHUNKS):
        column = call(
            functools.partial(column_kernel, rows=rows), [shape((rows + PAD, dval), BF16)], sent[i], f"column{i}"
        )[0]
        columns.append(
            [lax.ppermute(column, "seq", [(j, j + k) for j in range(spans - k)]) for k in range(1, spans)]
        )
    parts = []
    for i in range(CHUNKS):
        pres = call(
            functools.partial(prefix_kernel, rows=rows, nz=nz, spans=spans - 1),
            [shape((rows, dval), BF16)] * nz,
            list(sent[i]) + columns[i],
            f"prefix{i}",
            [
                pltpu.VMEM((nz, rows, dval), F32),
                pltpu.VMEM((nz, 8, dval), F32),
                pltpu.VMEM((nz, rows, dval), BF16),
            ],
        )
        parts.append([pres[0]] + [turn(pres[k], k) for k in range(1, nz)])
    out = None
    for i, (first, own, rec) in enumerate(chunks):
        if out is not None:
            own = after(own, out)
        mine, other = call(
            functools.partial(spread_kernel, first=first, half=half, dkey=dkey, rows=rows, nz=nz),
            [shape((per * dkey, dval), BF16)] * 2,
            parts[i] + [own, rec, total, rtotal],
            f"spread{i}",
        )
        back = lax.ppermute(other, "core", swap)
        for where, memory, name in ((first, mine, "own"), (half + first, back, "other")):
            out = final(
                scal, qproj, memory, intra, cols, ogate, gain, out,
                first=where, per=per, half=half, dval=dval, name=f"final_{name}{i}",
            )
    return out


def solution(mesh):
    spans, lanes = mesh.shape["seq"], mesh.shape["hv"]
    inner = Mesh(mesh.devices.reshape(spans, lanes // CORES, CORES), ("seq", "z", "core"))
    split = P(("seq", "z", "core"), None)
    return jax.shard_map(
        shards, mesh=inner, in_specs=(split,) * 6 + (P(),), out_specs=split, check_vma=False
    )
```

```python
import functools
import math

import jax
import jax.numpy as jnp
from jax import lax
from jax.experimental import pallas as pl
from jax.experimental.pallas import tpu as pltpu
from jax.sharding import Mesh
from jax.sharding import PartitionSpec as P


F32 = jnp.float32
BF16 = jnp.bfloat16
CORES = 2
PAD = 8
PIECES = 3
CHUNKS = 2


def call(kernel, outs, ins, scratch=()):
    vmem = pl.BlockSpec(memory_space=pltpu.VMEM)
    return pl.pallas_call(
        kernel,
        out_shape=outs,
        in_specs=[vmem] * len(ins),
        out_specs=[vmem] * len(outs),
        scratch_shapes=list(scratch),
        compiler_params=pltpu.CompilerParams(vmem_limit_bytes=8 << 20),
    )(*ins)


def shape(dims, dtype):
    return jax.ShapeDtypeStruct(dims, dtype)


def rows_at(start, size):
    return pl.ds(pl.multiple_of(start, size), size)


def head_cols(j, half, width):
    head = lax.rem(lax.axis_index("core") * half + j, CORES * half)
    return pl.ds(pl.multiple_of(head * width, width), width)


def first_kernel(ig, fg, q, k, v, rowa, cols, out, core, qv, kv, vv, igv, fgv, sems, *, scale, first, per):
    def block(source, target, i):
        width = source.shape[1] // (2 * first // per)
        at = lax.rem(lax.axis_index("core") * (first // per) + i, 2 * first // per)
        at = pl.ds(pl.multiple_of(at * width, width), width)
        return source.at[:, at], target.at[:, at]

    blocks = [first // per] + [i for i in range(2 * first // per) if i != first // per]
    sources = [(fg, fgv), (ig, igv)] + [block(*a, i) for i in blocks for a in ((k, kv), (v, vv))] + [(q, qv)]
    moves = [pltpu.make_async_copy(*pair, sems.at[i]) for i, pair in enumerate(sources)]
    for move in moves:
        move.start()
    heads, tok = igv.shape
    half = heads // CORES
    zero = lax.axis_index("core") == 0
    core[0] = lax.axis_index("core").astype(jnp.int32)
    earlier = lax.broadcasted_iota(jnp.int32, (tok, tok), 0)
    later = lax.broadcasted_iota(jnp.int32, (tok, tok), 1)
    tri = (earlier <= later).astype(F32).astype(BF16)
    own_first = lambda a: jnp.where(zero, a, jnp.concatenate([a[half:], a[:half]], axis=0))
    moves[0].wait()
    lf = own_first(jax.nn.log_sigmoid(fgv[...].astype(F32)))
    high = lf.astype(BF16)
    rest = lf - high.astype(F32)
    mid = rest.astype(BF16)
    low = (rest - mid.astype(F32)).astype(BF16)
    sums = lambda a: jnp.dot(a, tri, preferred_element_type=F32)
    g = sums(high) + sums(mid) + sums(low)
    last = g[:, tok - 1 : tok]
    moves[1].wait()
    il = own_first(15.0 * jnp.tanh(igv[...].astype(F32) / 15.0))
    rowa[...] = il - g
    cols[...] = jnp.concatenate([g, jnp.exp(last - g + il), jnp.exp(g) / scale], axis=0).T
    size = out.shape[0] - heads
    out[size:, :] = jnp.broadcast_to(last, (heads, out.shape[1]))
    moves[2].wait()
    moves[3].wait()
    state_body(kv, vv, cols, out, first=first, per=per, half=half, dkey=size // per)
    for move in moves[4:]:
        move.wait()


def state_body(k, v, cols, out, *, first, per, half, dkey):
    heads, dval = CORES * half, out.shape[1]
    dims = (((0,), (0,)), ((), ()))
    for j in range(per):
        weight = cols[:, heads + first + j : heads + first + j + 1]
        kw = k[:, head_cols(first + j, half, dkey)].astype(F32) * weight
        high = kw.astype(BF16)
        low = (kw - high.astype(F32)).astype(BF16)
        value = v[:, head_cols(first + j, half, dval)]
        part = lax.dot_general(high, value, dims, preferred_element_type=F32)
        out[j * dkey : (j + 1) * dkey, :] = part + lax.dot_general(low, value, dims, preferred_element_type=F32)


def state_kernel(k, v, cols, out, *, first, per, half):
    state_body(k, v, cols, out, first=first, per=per, half=half, dkey=out.shape[0] // per)


def put_logs(ref, start, values):
    rows = lax.broadcasted_iota(jnp.int32, (PAD, ref.shape[1]), 0)
    tile = jnp.zeros((PAD, ref.shape[1]), F32)
    for i, value in enumerate(values):
        high = value.astype(BF16).astype(F32)
        mid = (value - high).astype(BF16).astype(F32)
        for j, piece in enumerate((high, mid, value - high - mid)):
            tile = jnp.where(rows == PIECES * i + j, piece, tile)
    ref[start:, :] = tile.astype(BF16)


def get_log(ref, start, i):
    tile = ref[start:, :].astype(F32)
    rows = [tile[j : j + 1] for j in range(PIECES * i, PIECES * i + PIECES)]
    return rows[0] + rows[1] + rows[2]


def chip_kernel(own, rec, table, rtable, *msgs, chunk, per, half, dkey, rows):
    place, zero = lax.axis_index("z"), lax.axis_index("core") == 0
    base = table.shape[0] - CORES * half
    for k in range(len(msgs)):
        dest = place ^ k
        here = rows_at(dest * rows, rows)
        head = base + (dest * rows) // dkey
        logs = [
            (table[pl.ds(head + i * per, 1), :], rtable[pl.ds(head + i * per + half, 1), :]) for i in range(CHUNKS)
        ]
        ga, gb = logs[chunk]
        decay = jnp.exp(jnp.where(zero, gb, ga))
        a, b = own[here, :], rec[here, :]
        state = decay * jnp.where(zero, a, b) + jnp.where(zero, b, a)
        msgs[k][0:rows, :] = state.astype(BF16)
        if chunk == 0:
            put_logs(msgs[k], rows, [x + y for x, y in logs])


def column_kernel(*refs, rows, nz, chunk):
    msgs, heads, out = refs[:nz], refs[-1 - nz : -1], refs[-1]
    place = lax.axis_index("z")
    logs = [[get_log(m, rows, i) for m in heads] for i in (range(CHUNKS) if chunk == 0 else [chunk])]
    own = logs[0]
    places = [place ^ k for k in range(nz)]
    total = jnp.zeros((rows, out.shape[1]), F32)
    for k in range(nz):
        behind = jnp.zeros_like(own[0])
        for j in range(nz):
            if j != k:
                behind = behind + jnp.where(places[j] > places[k], own[j], 0.0)
        total = total + jnp.exp(behind) * msgs[k][0:rows, :].astype(F32)
    out[0:rows, :] = total.astype(BF16)
    if chunk == 0:
        put_logs(out, rows, [functools.reduce(lambda x, y: x + y, log) for log in logs])


def prefix_kernel(*refs, rows, nz, spans, chunk):
    count = nz + spans - 1
    msgs, cols = refs[:nz], refs[nz:count]
    if chunk:
        heads, rheads, refs = refs[count : count + nz], refs[count + nz : 2 * count], refs[2 * count :]
    else:
        heads, rheads, refs = msgs, cols, refs[count:]
    outs = refs[:nz]
    states, logs, pres = refs[nz:]
    place, span = lax.axis_index("z"), lax.axis_index("seq")
    for k in range(nz):
        states[place ^ k] = msgs[k][0:rows, :].astype(F32)
        logs[place ^ k] = jnp.broadcast_to(get_log(heads[k], rows, chunk), logs.shape[1:])
    state = jnp.zeros(states.shape[1:], F32)
    earlier = [span ^ k for k in range(1, spans)]
    decays = [jnp.where(s < span, get_log(head, rows, chunk), 0.0) for s, head in zip(earlier, rheads)]
    for s, col in zip(earlier, cols):
        behind = jnp.zeros_like(decays[0])
        for t, decay in zip(earlier, decays):
            behind = behind + jnp.where(t > s, decay, 0.0)
        state = state + jnp.where(s < span, jnp.exp(behind) * col[0:rows, :].astype(F32), 0.0)
    for z in range(nz):
        pres[z] = state.astype(BF16)
        state = jnp.exp(logs[z][0:1, :]) * state + states[z]
    for k in range(nz):
        outs[k][...] = pres[place ^ k]


def spread_kernel(*refs, first, half, dkey, rows, nz):
    parts = refs[:nz]
    own, rec, table, rtable, mine, other = refs[nz:]
    place, zero = lax.axis_index("z"), lax.axis_index("core") == 0
    base = table.shape[0] - CORES * half
    for k in range(nz):
        source = place ^ k
        here = rows_at(source * rows, rows)
        head = base + first + (source * rows) // dkey
        decay = jnp.exp(jnp.where(zero, table[pl.ds(head, 1), :], rtable[pl.ds(head + half, 1), :]))
        before = parts[k][...].astype(F32)
        behind = decay * before + jnp.where(zero, own[here, :], rec[here, :])
        mine[here, :] = jnp.where(zero, before, behind).astype(BF16)
        other[here, :] = jnp.where(zero, behind, before).astype(BF16)


def gate_kernel(og, gain, out, *, half, dval):
    for j in range(CORES * half):
        at = head_cols(j, half, dval)
        out[:, j * dval : (j + 1) * dval] = gain[:, at].astype(F32) * jax.nn.sigmoid(og[:, at].astype(F32))


def intra_kernel(q, k, v, rowa, cols, out, *, half, dkey, dval, scale):
    tok = q.shape[0]
    rows = lax.broadcasted_iota(jnp.int32, (tok, tok), 0)
    lanes = lax.broadcasted_iota(jnp.int32, (tok, tok), 1)
    causal = lanes <= rows
    for j in range(CORES * half):
        at = head_cols(j, half, dkey)
        scores = lax.dot_general(q[:, at], k[:, at], (((1,), (1,)), ((), ())), preferred_element_type=F32)
        logw = jnp.where(causal, cols[:, j : j + 1] + rowa[j : j + 1, :], -jnp.inf)
        prod = (scores / scale * jnp.exp(logw)).astype(BF16)
        out[:, j * dval : (j + 1) * dval] = jnp.dot(
            prod, v[:, head_cols(j, half, dval)], preferred_element_type=F32
        )


def final_kernel(core, q, state, intra, cols, gate, *rest, first, per, half):
    out = rest[-1]
    heads = CORES * half
    dkey, dval = state.shape[0] // per, state.shape[1]
    for j in range(per):
        head = first + j
        here = slice(head * dval, (head + 1) * dval)
        inter = jnp.dot(
            q[:, head_cols(head, half, dkey)], state[j * dkey : (j + 1) * dkey, :], preferred_element_type=F32
        )
        decay = cols[:, 2 * heads + head : 2 * heads + head + 1]
        hval = (intra[:, here] + decay * inter).astype(BF16).astype(F32)
        meansq = jnp.mean(hval * hval, axis=1, keepdims=True)
        normed = hval * lax.rsqrt(meansq + 1e-06)
        out[:, j * dval : (j + 1) * dval] = (normed * gate[:, here]).astype(BF16)


def final(core, q, state, intra, cols, gate, out, *, first, per, half, dval):
    tok = q.shape[0]
    blocks = CORES * half // per
    at = lambda j, s: (0, lax.rem(s[0] * (half // per) + first // per, blocks))
    vmem = pl.BlockSpec(memory_space=pltpu.VMEM)
    ins = [q, state, intra, cols, gate]
    specs = [vmem] * len(ins)
    aliases = {}
    if out is not None:
        ins.append(out)
        specs.append(pl.BlockSpec(memory_space=pl.ANY))
        aliases = {len(ins): 0}
    return pl.pallas_call(
        functools.partial(final_kernel, first=first, per=per, half=half),
        out_shape=shape((tok, CORES * half * dval), BF16),
        grid_spec=pltpu.PrefetchScalarGridSpec(
            num_scalar_prefetch=1,
            grid=(1,),
            in_specs=specs,
            out_specs=pl.BlockSpec((tok, per * dval), at),
        ),
        input_output_aliases=aliases,
        compiler_params=pltpu.CompilerParams(vmem_limit_bytes=8 << 20),
    )(core, *ins)


def after(value, *others):
    return lax.optimization_barrier((value,) + others)[0]


def shards(qproj, kproj, vproj, igate, fgate, ogate, norm_gain):
    spans, nz = lax.axis_size("seq"), lax.axis_size("z")
    tok, heads = igate.shape
    dkey = qproj.shape[1] // heads
    dval = vproj.shape[1] // heads
    half = heads // CORES
    per = half // CHUNKS
    rows = per * dkey // nz
    assert rows % PAD == 0 and dkey % rows == 0 and PIECES * CHUNKS <= PAD
    assert nz & (nz - 1) == 0 and spans & (spans - 1) == 0
    scale = math.sqrt(dkey)

    def swap(a, axis, bit, up=False):
        pairs = [(j, j ^ bit) for j in range(lax.axis_size(axis)) if not up or j < j ^ bit]
        return lax.ppermute(a, axis, pairs)

    vmem, hbm = pl.BlockSpec(memory_space=pltpu.VMEM), pl.BlockSpec(memory_space=pltpu.HBM)
    loads = [shape(qproj.shape, BF16), shape(kproj.shape, BF16), shape(vproj.shape, BF16)]
    rowa, cols, table, core, qvm, kvm, vvm = pl.pallas_call(
        functools.partial(first_kernel, scale=scale, first=half, per=per),
        out_shape=[
            shape((heads, tok), F32),
            shape((tok, 3 * heads), F32),
            shape((per * dkey + heads, dval), F32),
            shape((1,), jnp.int32),
        ] + loads,
        in_specs=[hbm] * 5,
        out_specs=[vmem, vmem, vmem, pl.BlockSpec(memory_space=pltpu.SMEM), vmem, vmem, vmem],
        scratch_shapes=[
            pltpu.VMEM((heads, tok), BF16),
            pltpu.VMEM((heads, tok), BF16),
            pltpu.SemaphoreType.DMA((3 + 2 * CORES * CHUNKS,)),
        ],
        compiler_params=pltpu.CompilerParams(vmem_limit_bytes=8 << 20),
        name="first",
    )(*(pltpu.with_memory_space_constraint(a, pltpu.HBM) for a in (igate.T, fgate.T, qproj, kproj, vproj)))

    def state(first):
        return call(
            functools.partial(state_kernel, first=first, per=per, half=half),
            [shape((per * dkey, dval), F32)],
            [kvm, vvm, cols],
        )[0]

    others = [table] + [state(half + i * per) for i in range(1, CHUNKS)]
    recs = [swap(other, "core", 1) for other in others]
    owns = [state(i * per) for i in range(CHUNKS)]
    rtable = recs[0]

    pads = [PAD] + [0] * (CHUNKS - 1)
    sent = []
    for i in range(CHUNKS):
        msgs = call(
            functools.partial(chip_kernel, chunk=i, per=per, half=half, dkey=dkey, rows=rows),
            [shape((rows + pads[i], dval), BF16)] * nz,
            [owns[i], recs[i], table, rtable],
        )
        sent.append([msgs[0]] + [swap(msgs[k], "z", k) for k in range(1, nz)])

    gate = call(
        functools.partial(gate_kernel, half=half, dval=dval),
        [shape((tok, heads * dval), F32)],
        [ogate, norm_gain.reshape(1, heads * dval)],
    )[0]
    intra = call(
        functools.partial(intra_kernel, half=half, dkey=dkey, dval=dval, scale=scale),
        [shape((tok, heads * dval), F32)],
        [qvm, kvm, vvm, rowa, after(cols, sent[-1][0])],
    )[0]
    sent[0][0] = after(sent[0][0], intra, gate)

    parts, cumuls = [], []
    for i in range(CHUNKS):
        total = call(
            functools.partial(column_kernel, rows=rows, nz=nz, chunk=i),
            [shape((rows + pads[i], dval), BF16)],
            sent[i] + (sent[0] if i else []),
        )[0]
        cumuls.append([swap(total, "seq", k, up=True) for k in range(1, spans)])
        pres = call(
            functools.partial(prefix_kernel, rows=rows, nz=nz, spans=spans, chunk=i),
            [shape((rows, dval), BF16)] * nz,
            sent[i] + cumuls[i] + (sent[0] + cumuls[0] if i else []),
            [
                pltpu.VMEM((nz, rows, dval), F32),
                pltpu.VMEM((nz, 8, dval), F32),
                pltpu.VMEM((nz, rows, dval), BF16),
            ],
        )
        parts.append([pres[0]] + [swap(pres[k], "z", k) for k in range(1, nz)])
    out = None
    for i in range(CHUNKS):
        own = owns[i] if out is None else after(owns[i], out)
        mine, other = call(
            functools.partial(spread_kernel, first=i * per, half=half, dkey=dkey, rows=rows, nz=nz),
            [shape((per * dkey, dval), BF16)] * 2,
            parts[i] + [own, recs[i], table, rtable],
        )
        back = swap(other, "core", 1)
        for where, memory in ((i * per, mine), (half + i * per, back)):
            out = final(
                core, qvm, memory, intra, cols, gate, out,
                first=where, per=per, half=half, dval=dval,
            )
    return out


def solution(mesh):
    spans, lanes = mesh.shape["seq"], mesh.shape["hv"]
    nz = lanes // CORES
    inner = Mesh(mesh.devices.reshape(spans, nz, CORES), ("seq", "z", "core"))
    split = P(("seq", "z", "core"), None)

    return jax.shard_map(shards, mesh=inner, in_specs=(split,) * 6 + (P(),), out_specs=split, check_vma=False)
```

```python
import functools
import math

import jax
import jax.numpy as jnp
from jax import lax
from jax.experimental import pallas as pl
from jax.experimental.pallas import tpu as pltpu
from jax.sharding import Mesh
from jax.sharding import PartitionSpec as P


F32 = jnp.float32
BF16 = jnp.bfloat16
CORES = 2
PAD = 8
PIECES = 3
CHUNKS = 2


def call(kernel, outs, ins, scratch=()):
    vmem = pl.BlockSpec(memory_space=pltpu.VMEM)
    return pl.pallas_call(
        kernel,
        out_shape=outs,
        in_specs=[vmem] * len(ins),
        out_specs=[vmem] * len(outs),
        scratch_shapes=list(scratch),
        compiler_params=pltpu.CompilerParams(vmem_limit_bytes=8 << 20),
    )(*ins)


def shape(dims, dtype):
    return jax.ShapeDtypeStruct(dims, dtype)


def rows_at(start, size):
    return pl.ds(pl.multiple_of(start, size), size)


def head_cols(j, half, width):
    head = lax.rem(lax.axis_index("core") * half + j, CORES * half)
    return pl.ds(pl.multiple_of(head * width, width), width)


def first_kernel(ig, fg, q, k, v, rowa, cols, out, core, qv, kv, vv, igv, fgv, sems, *, scale, first, per):
    def block(source, target, i):
        width = source.shape[1] // (2 * first // per)
        at = lax.rem(lax.axis_index("core") * (first // per) + i, 2 * first // per)
        at = pl.ds(pl.multiple_of(at * width, width), width)
        return source.at[:, at], target.at[:, at]

    blocks = [first // per] + [i for i in range(2 * first // per) if i != first // per]
    sources = [(fg, fgv), (ig, igv)] + [block(*a, i) for i in blocks for a in ((k, kv), (v, vv))] + [(q, qv)]
    moves = [pltpu.make_async_copy(*pair, sems.at[i]) for i, pair in enumerate(sources)]
    for move in moves:
        move.start()
    heads, tok = igv.shape
    half = heads // CORES
    zero = lax.axis_index("core") == 0
    core[0] = lax.axis_index("core").astype(jnp.int32)
    earlier = lax.broadcasted_iota(jnp.int32, (tok, tok), 0)
    later = lax.broadcasted_iota(jnp.int32, (tok, tok), 1)
    tri = (earlier <= later).astype(F32).astype(BF16)
    own_first = lambda a: jnp.where(zero, a, jnp.concatenate([a[half:], a[:half]], axis=0))
    moves[0].wait()
    lf = own_first(jax.nn.log_sigmoid(fgv[...].astype(F32)))
    high = lf.astype(BF16)
    rest = lf - high.astype(F32)
    mid = rest.astype(BF16)
    low = (rest - mid.astype(F32)).astype(BF16)
    sums = lambda a: jnp.dot(a, tri, preferred_element_type=F32)
    g = sums(high) + sums(mid) + sums(low)
    last = g[:, tok - 1 : tok]
    moves[1].wait()
    il = own_first(15.0 * jnp.tanh(igv[...].astype(F32) / 15.0))
    rowa[...] = il - g
    cols[...] = jnp.concatenate([g, jnp.exp(last - g + il), jnp.exp(g) / scale], axis=0).T
    size = out.shape[0] - heads
    out[size:, :] = jnp.broadcast_to(last, (heads, out.shape[1]))
    moves[2].wait()
    moves[3].wait()
    state_body(kv, vv, cols, out, first=first, per=per, half=half, dkey=size // per)
    for move in moves[4:]:
        move.wait()


def state_body(k, v, cols, out, *, first, per, half, dkey):
    heads, dval = CORES * half, out.shape[1]
    dims = (((0,), (0,)), ((), ()))
    for j in range(per):
        weight = cols[:, heads + first + j : heads + first + j + 1]
        kw = k[:, head_cols(first + j, half, dkey)].astype(F32) * weight
        high = kw.astype(BF16)
        low = (kw - high.astype(F32)).astype(BF16)
        value = v[:, head_cols(first + j, half, dval)]
        part = lax.dot_general(high, value, dims, preferred_element_type=F32)
        out[j * dkey : (j + 1) * dkey, :] = part + lax.dot_general(low, value, dims, preferred_element_type=F32)


def state_kernel(k, v, cols, out, *, first, per, half):
    state_body(k, v, cols, out, first=first, per=per, half=half, dkey=out.shape[0] // per)


def put_logs(ref, start, values):
    rows = lax.broadcasted_iota(jnp.int32, (PAD, ref.shape[1]), 0)
    tile = jnp.zeros((PAD, ref.shape[1]), F32)
    for i, value in enumerate(values):
        high = value.astype(BF16).astype(F32)
        mid = (value - high).astype(BF16).astype(F32)
        for j, piece in enumerate((high, mid, value - high - mid)):
            tile = jnp.where(rows == PIECES * i + j, piece, tile)
    ref[start:, :] = tile.astype(BF16)


def get_log(ref, start, i):
    tile = ref[start:, :].astype(F32)
    rows = [tile[j : j + 1] for j in range(PIECES * i, PIECES * i + PIECES)]
    return rows[0] + rows[1] + rows[2]


def chip_kernel(own, rec, table, rtable, *msgs, chunk, per, half, dkey, rows):
    place, zero = lax.axis_index("z"), lax.axis_index("core") == 0
    base = table.shape[0] - CORES * half
    for k in range(len(msgs)):
        dest = place ^ k
        here = rows_at(dest * rows, rows)
        head = base + (dest * rows) // dkey
        logs = [
            (table[pl.ds(head + i * per, 1), :], rtable[pl.ds(head + i * per + half, 1), :]) for i in range(CHUNKS)
        ]
        ga, gb = logs[chunk]
        decay = jnp.exp(jnp.where(zero, gb, ga))
        a, b = own[here, :], rec[here, :]
        state = decay * jnp.where(zero, a, b) + jnp.where(zero, b, a)
        msgs[k][0:rows, :] = state.astype(BF16)
        if chunk == 0:
            put_logs(msgs[k], rows, [x + y for x, y in logs])


def column_kernel(*refs, rows, nz, chunk):
    msgs, heads, out = refs[:nz], refs[-1 - nz : -1], refs[-1]
    place = lax.axis_index("z")
    logs = [[get_log(m, rows, i) for m in heads] for i in (range(CHUNKS) if chunk == 0 else [chunk])]
    own = logs[0]
    places = [place ^ k for k in range(nz)]
    total = jnp.zeros((rows, out.shape[1]), F32)
    for k in range(nz):
        behind = jnp.zeros_like(own[0])
        for j in range(nz):
            if j != k:
                behind = behind + jnp.where(places[j] > places[k], own[j], 0.0)
        total = total + jnp.exp(behind) * msgs[k][0:rows, :].astype(F32)
    out[0:rows, :] = total.astype(BF16)
    if chunk == 0:
        put_logs(out, rows, [functools.reduce(lambda x, y: x + y, log) for log in logs])


def prefix_kernel(*refs, rows, nz, spans, chunk):
    count = nz + spans - 1
    msgs, cols = refs[:nz], refs[nz:count]
    if chunk:
        heads, rheads, refs = refs[count : count + nz], refs[count + nz : 2 * count], refs[2 * count :]
    else:
        heads, rheads, refs = msgs, cols, refs[count:]
    outs = refs[:nz]
    states, logs, pres = refs[nz:]
    place, span = lax.axis_index("z"), lax.axis_index("seq")
    for k in range(nz):
        states[place ^ k] = msgs[k][0:rows, :].astype(F32)
        logs[place ^ k] = jnp.broadcast_to(get_log(heads[k], rows, chunk), logs.shape[1:])
    state = jnp.zeros(states.shape[1:], F32)
    earlier = [span ^ k for k in range(1, spans)]
    decays = [jnp.where(s < span, get_log(head, rows, chunk), 0.0) for s, head in zip(earlier, rheads)]
    for s, col in zip(earlier, cols):
        behind = jnp.zeros_like(decays[0])
        for t, decay in zip(earlier, decays):
            behind = behind + jnp.where(t > s, decay, 0.0)
        state = state + jnp.where(s < span, jnp.exp(behind) * col[0:rows, :].astype(F32), 0.0)
    for z in range(nz):
        pres[z] = state.astype(BF16)
        state = jnp.exp(logs[z][0:1, :]) * state + states[z]
    for k in range(nz):
        outs[k][...] = pres[place ^ k]


def spread_kernel(*refs, first, half, dkey, rows, nz):
    parts = refs[:nz]
    own, rec, table, rtable, mine, other = refs[nz:]
    place, zero = lax.axis_index("z"), lax.axis_index("core") == 0
    base = table.shape[0] - CORES * half
    for k in range(nz):
        source = place ^ k
        here = rows_at(source * rows, rows)
        head = base + first + (source * rows) // dkey
        decay = jnp.exp(jnp.where(zero, table[pl.ds(head, 1), :], rtable[pl.ds(head + half, 1), :]))
        before = parts[k][...].astype(F32)
        behind = decay * before + jnp.where(zero, own[here, :], rec[here, :])
        mine[here, :] = jnp.where(zero, before, behind).astype(BF16)
        other[here, :] = jnp.where(zero, behind, before).astype(BF16)


def gate_kernel(og, gain, out, *, half, dval):
    for j in range(CORES * half):
        at = head_cols(j, half, dval)
        out[:, j * dval : (j + 1) * dval] = gain[:, at].astype(F32) * jax.nn.sigmoid(og[:, at].astype(F32))


def intra_kernel(q, k, v, rowa, cols, out, *, half, dkey, dval, scale):
    tok = q.shape[0]
    rows = lax.broadcasted_iota(jnp.int32, (tok, tok), 0)
    lanes = lax.broadcasted_iota(jnp.int32, (tok, tok), 1)
    causal = lanes <= rows
    for j in range(CORES * half):
        at = head_cols(j, half, dkey)
        scores = lax.dot_general(q[:, at], k[:, at], (((1,), (1,)), ((), ())), preferred_element_type=F32)
        logw = jnp.where(causal, cols[:, j : j + 1] + rowa[j : j + 1, :], -jnp.inf)
        prod = (scores / scale * jnp.exp(logw)).astype(BF16)
        out[:, j * dval : (j + 1) * dval] = jnp.dot(
            prod, v[:, head_cols(j, half, dval)], preferred_element_type=F32
        )


def final_kernel(core, q, state, intra, cols, gate, *rest, first, per, half):
    out = rest[-1]
    heads = CORES * half
    dkey, dval = state.shape[0] // per, state.shape[1]
    for j in range(per):
        head = first + j
        here = slice(head * dval, (head + 1) * dval)
        inter = jnp.dot(
            q[:, head_cols(head, half, dkey)], state[j * dkey : (j + 1) * dkey, :], preferred_element_type=F32
        )
        decay = cols[:, 2 * heads + head : 2 * heads + head + 1]
        hval = (intra[:, here] + decay * inter).astype(BF16).astype(F32)
        meansq = jnp.mean(hval * hval, axis=1, keepdims=True)
        normed = hval * lax.rsqrt(meansq + 1e-06)
        out[:, j * dval : (j + 1) * dval] = (normed * gate[:, here]).astype(BF16)


def final(core, q, state, intra, cols, gate, out, *, first, per, half, dval):
    tok = q.shape[0]
    blocks = CORES * half // per
    at = lambda j, s: (0, lax.rem(s[0] * (half // per) + first // per, blocks))
    vmem = pl.BlockSpec(memory_space=pltpu.VMEM)
    ins = [q, state, intra, cols, gate]
    specs = [vmem] * len(ins)
    aliases = {}
    if out is not None:
        ins.append(out)
        specs.append(pl.BlockSpec(memory_space=pl.ANY))
        aliases = {len(ins): 0}
    return pl.pallas_call(
        functools.partial(final_kernel, first=first, per=per, half=half),
        out_shape=shape((tok, CORES * half * dval), BF16),
        grid_spec=pltpu.PrefetchScalarGridSpec(
            num_scalar_prefetch=1,
            grid=(1,),
            in_specs=specs,
            out_specs=pl.BlockSpec((tok, per * dval), at),
        ),
        input_output_aliases=aliases,
        compiler_params=pltpu.CompilerParams(vmem_limit_bytes=8 << 20),
    )(core, *ins)


def after(value, *others):
    return lax.optimization_barrier((value,) + others)[0]


def shards(qproj, kproj, vproj, igate, fgate, ogate, norm_gain):
    spans, nz = lax.axis_size("seq"), lax.axis_size("z")
    tok, heads = igate.shape
    dkey = qproj.shape[1] // heads
    dval = vproj.shape[1] // heads
    half = heads // CORES
    per = half // CHUNKS
    rows = per * dkey // nz
    assert rows % PAD == 0 and dkey % rows == 0 and PIECES * CHUNKS <= PAD
    assert nz & (nz - 1) == 0 and spans & (spans - 1) == 0
    scale = math.sqrt(dkey)

    def swap(a, axis, bit):
        pairs = [(j, j ^ bit) for j in range(lax.axis_size(axis))]
        return lax.ppermute(a, axis, pairs)

    vmem, hbm = pl.BlockSpec(memory_space=pltpu.VMEM), pl.BlockSpec(memory_space=pltpu.HBM)
    loads = [shape(qproj.shape, BF16), shape(kproj.shape, BF16), shape(vproj.shape, BF16)]
    rowa, cols, table, core, qvm, kvm, vvm = pl.pallas_call(
        functools.partial(first_kernel, scale=scale, first=half, per=per),
        out_shape=[
            shape((heads, tok), F32),
            shape((tok, 3 * heads), F32),
            shape((per * dkey + heads, dval), F32),
            shape((1,), jnp.int32),
        ] + loads,
        in_specs=[hbm] * 5,
        out_specs=[vmem, vmem, vmem, pl.BlockSpec(memory_space=pltpu.SMEM), vmem, vmem, vmem],
        scratch_shapes=[
            pltpu.VMEM((heads, tok), BF16),
            pltpu.VMEM((heads, tok), BF16),
            pltpu.SemaphoreType.DMA((3 + 2 * CORES * CHUNKS,)),
        ],
        compiler_params=pltpu.CompilerParams(vmem_limit_bytes=8 << 20),
        name="first",
    )(*(pltpu.with_memory_space_constraint(a, pltpu.HBM) for a in (igate.T, fgate.T, qproj, kproj, vproj)))

    def state(first):
        return call(
            functools.partial(state_kernel, first=first, per=per, half=half),
            [shape((per * dkey, dval), F32)],
            [kvm, vvm, cols],
        )[0]

    others = [table] + [state(half + i * per) for i in range(1, CHUNKS)]
    recs = [swap(other, "core", 1) for other in others]
    owns = [state(i * per) for i in range(CHUNKS)]
    rtable = recs[0]

    pads = [PAD] + [0] * (CHUNKS - 1)
    sent = []
    for i in range(CHUNKS):
        msgs = call(
            functools.partial(chip_kernel, chunk=i, per=per, half=half, dkey=dkey, rows=rows),
            [shape((rows + pads[i], dval), BF16)] * nz,
            [owns[i], recs[i], table, rtable],
        )
        sent.append([msgs[0]] + [swap(msgs[k], "z", k) for k in range(1, nz)])

    gate = call(
        functools.partial(gate_kernel, half=half, dval=dval),
        [shape((tok, heads * dval), F32)],
        [ogate, norm_gain.reshape(1, heads * dval)],
    )[0]
    intra = call(
        functools.partial(intra_kernel, half=half, dkey=dkey, dval=dval, scale=scale),
        [shape((tok, heads * dval), F32)],
        [qvm, kvm, vvm, rowa, after(cols, sent[-1][0])],
    )[0]
    sent[0][0] = after(sent[0][0], intra, gate)

    parts, cumuls = [], []
    for i in range(CHUNKS):
        total = call(
            functools.partial(column_kernel, rows=rows, nz=nz, chunk=i),
            [shape((rows + pads[i], dval), BF16)],
            sent[i] + (sent[0] if i else []),
        )[0]
        cumuls.append([swap(total, "seq", k) for k in range(1, spans)])
        pres = call(
            functools.partial(prefix_kernel, rows=rows, nz=nz, spans=spans, chunk=i),
            [shape((rows, dval), BF16)] * nz,
            sent[i] + cumuls[i] + (sent[0] + cumuls[0] if i else []),
            [
                pltpu.VMEM((nz, rows, dval), F32),
                pltpu.VMEM((nz, 8, dval), F32),
                pltpu.VMEM((nz, rows, dval), BF16),
            ],
        )
        parts.append([pres[0]] + [swap(pres[k], "z", k) for k in range(1, nz)])
    out = None
    for i in range(CHUNKS):
        own = owns[i] if out is None else after(owns[i], out)
        mine, other = call(
            functools.partial(spread_kernel, first=i * per, half=half, dkey=dkey, rows=rows, nz=nz),
            [shape((per * dkey, dval), BF16)] * 2,
            parts[i] + [own, recs[i], table, rtable],
        )
        back = swap(other, "core", 1)
        for where, memory in ((i * per, mine), (half + i * per, back)):
            out = final(
                core, qvm, memory, intra, cols, gate, out,
                first=where, per=per, half=half, dval=dval,
            )
    return out


def solution(mesh):
    spans, lanes = mesh.shape["seq"], mesh.shape["hv"]
    nz = lanes // CORES
    inner = Mesh(mesh.devices.reshape(spans, nz, CORES), ("seq", "z", "core"))
    split = P(("seq", "z", "core"), None)

    return jax.shard_map(shards, mesh=inner, in_specs=(split,) * 6 + (P(),), out_specs=split, check_vma=False)
```

```python
import functools
import math

import jax
import jax.numpy as jnp
from jax import lax
from jax.experimental import pallas as pl
from jax.experimental.pallas import tpu as pltpu
from jax.sharding import Mesh
from jax.sharding import PartitionSpec as P


F32 = jnp.float32
BF16 = jnp.bfloat16
CORES = 2
SHARES = (2, 2)
CHUNKS = len(SHARES)
PIECES = 2
PAD = 8


def call(kernel, outs, ins, scratch=()):
    vmem = pl.BlockSpec(memory_space=pltpu.VMEM)
    return pl.pallas_call(
        kernel,
        out_shape=outs,
        in_specs=[vmem] * len(ins),
        out_specs=[vmem] * len(outs),
        scratch_shapes=list(scratch),
        compiler_params=pltpu.CompilerParams(vmem_limit_bytes=8 << 20),
    )(*ins)


def shape(dims, dtype):
    return jax.ShapeDtypeStruct(dims, dtype)


def rows_at(start, size):
    return pl.ds(pl.multiple_of(start, size), size)


def head_cols(j, half, width):
    head = lax.rem(lax.axis_index("core") * half + j, CORES * half)
    return pl.ds(pl.multiple_of(head * width, width), width)


def column_block(source, target, first, per, heads):
    width = source.shape[1] // heads
    at = lax.rem(lax.axis_index("core") * (heads // CORES) + first, heads)
    at = pl.ds(pl.multiple_of(at * width, width), per * width)
    return source.at[:, at], target.at[:, at]


def first_kernel(ig, fg, k, v, rowa, cols, out, kv, vv, igv, fgv, sems, *, scale, first, per):
    heads, tok = igv.shape
    half = heads // CORES
    blocks = [column_block(*a, first, per, heads) for a in ((k, kv), (v, vv))]
    moves = [
        pltpu.make_async_copy(*pair, sems.at[i]) for i, pair in enumerate([(fg, fgv), (ig, igv)] + blocks)
    ]
    for move in moves:
        move.start()
    zero = lax.axis_index("core") == 0
    earlier = lax.broadcasted_iota(jnp.int32, (tok, tok), 0)
    later = lax.broadcasted_iota(jnp.int32, (tok, tok), 1)
    tri = (earlier <= later).astype(F32).astype(BF16)
    own_first = lambda a: jnp.where(zero, a, jnp.concatenate([a[half:], a[:half]], axis=0))
    moves[0].wait()
    lf = own_first(jax.nn.log_sigmoid(fgv[...].astype(F32)))
    high = lf.astype(BF16)
    rest = lf - high.astype(F32)
    mid = rest.astype(BF16)
    low = (rest - mid.astype(F32)).astype(BF16)
    sums = lambda a: jnp.dot(a, tri, preferred_element_type=F32)
    g = sums(high) + sums(mid) + sums(low)
    last = g[:, tok - 1 : tok]
    moves[1].wait()
    il = own_first(15.0 * jnp.tanh(igv[...].astype(F32) / 15.0))
    rowa[...] = il - g
    cols[...] = jnp.concatenate([g, jnp.exp(last - g + il), jnp.exp(g) / scale], axis=0).T
    size = out.shape[0] - heads
    out[size:, :] = jnp.broadcast_to(last, (heads, out.shape[1]))
    moves[2].wait()
    moves[3].wait()
    state_body(kv, vv, cols, out, first=first, per=per, half=half, dkey=size // per)


def early_kernel(k, v, cols, *refs, stretches, half, dkey):
    outs, (kv, vv, sems) = refs[:-3], refs[-3:]
    pairs = ((k, kv), (v, vv))
    sources = [column_block(*a, *where, CORES * half) for where in stretches for a in pairs]
    moves = [pltpu.make_async_copy(*pair, sems.at[i]) for i, pair in enumerate(sources)]
    for move in moves:
        move.start()
    for i, (out, (first, per)) in enumerate(zip(outs, stretches)):
        moves[2 * i].wait()
        moves[2 * i + 1].wait()
        state_body(kv, vv, cols, out, first=first, per=per, half=half, dkey=dkey)


def rest_kernel(q, k, v, cols, *refs, stretches, built, half, dkey):
    outs, (qv, kv, vv, sems) = refs[:-4], refs[-4:]
    pairs = ((k, kv), (v, vv))
    sources = [column_block(*a, *where, CORES * half) for where in stretches for a in pairs]
    moves = [pltpu.make_async_copy(*pair, sems.at[i]) for i, pair in enumerate(sources + [(q, qv)])]
    for move in moves:
        move.start()
    for i, (out, (first, per)) in enumerate(zip(outs, stretches[:built])):
        moves[2 * i].wait()
        moves[2 * i + 1].wait()
        state_body(kv, vv, cols, out, first=first, per=per, half=half, dkey=dkey)
    for move in moves[2 * built :]:
        move.wait()


def state_body(k, v, cols, out, *, first, per, half, dkey):
    heads, dval = CORES * half, out.shape[1]
    dims = (((0,), (0,)), ((), ()))
    for j in range(per):
        weight = cols[:, heads + first + j : heads + first + j + 1]
        kw = k[:, head_cols(first + j, half, dkey)].astype(F32) * weight
        high = kw.astype(BF16)
        low = (kw - high.astype(F32)).astype(BF16)
        value = v[:, head_cols(first + j, half, dval)]
        part = lax.dot_general(high, value, dims, preferred_element_type=F32)
        out[j * dkey : (j + 1) * dkey, :] = part + lax.dot_general(low, value, dims, preferred_element_type=F32)


def put_logs(ref, values):
    rows = lax.broadcasted_iota(jnp.int32, (PAD, ref.shape[1]), 0)
    tile = jnp.zeros((PAD, ref.shape[1]), F32)
    for i, value in enumerate(values):
        high = value.astype(BF16).astype(F32)
        for j, piece in enumerate((high, value - high)):
            tile = jnp.where(rows == PIECES * i + j, piece, tile)
    ref[ref.shape[0] - PAD :, :] = tile.astype(BF16)


def get_log(ref, i):
    tile = ref[ref.shape[0] - PAD :, :].astype(F32)
    return tile[PIECES * i : PIECES * i + 1] + tile[PIECES * i + 1 : PIECES * i + 2]


def pair_of(mine, theirs, bit, axis="z"):
    behind = (lax.axis_index(axis) & bit) != 0
    return jnp.where(behind, theirs, mine), jnp.where(behind, mine, theirs)


def halves(bit):
    side = (lax.axis_index("z") & bit) // bit
    return side, 1 - side


def chip_kernel(own, rec, table, rtable, keep, send, *logs_out, chunk, firsts, sizes, half, dkey):
    rows = keep.shape[0]
    base = table.shape[0] - CORES * half
    for where, target in zip(halves(1), (keep, send)):
        here = rows_at(where * rows, rows)
        heads = [base + first + (where * size) // dkey for first, size in zip(firsts, sizes)]
        logs = [(table[pl.ds(head, 1), :], rtable[pl.ds(head + half, 1), :]) for head in heads]
        decay = jnp.exp(pair_of(*logs[chunk], 1, "core")[1])
        early, late = pair_of(own[here, :], rec[here, :], 1, "core")
        target[0:rows, :] = (decay * early + late).astype(target.dtype)
        if chunk == 0:
            sums = [x + y for x, y in logs]
            if target is send:
                put_logs(send, sums)
            else:
                for i, value in enumerate(sums):
                    logs_out[0][i : i + 1, :] = value


def up_kernel(*refs, bit, chunk):
    if chunk:
        keep, recv, log, head = refs[:4]
        outs = refs[4:]
    else:
        keep, recv, log = refs[:3]
        head, outs = recv, refs[3:]
    rows = keep.shape[0]
    decay = jnp.exp(pair_of(log[chunk : chunk + 1, :], get_log(head, chunk), bit)[1])
    last = outs[0].shape[0] >= rows
    size = rows if last else rows // 2
    parts = [(0, outs[0])] if last else list(zip(halves(2 * bit), outs[:2]))
    for where, target in parts:
        here = slice(0, rows) if last else rows_at(where * size, size)
        early, late = pair_of(keep[here, :], recv[here, :].astype(F32), bit)
        target[0:size, :] = (decay * early + late).astype(target.dtype)
    if chunk == 0:
        sums = [log[i : i + 1, :] + get_log(head, i) for i in range(CHUNKS)]
        put_logs(outs[0] if last else outs[1], sums)
        if not last:
            for i, value in enumerate(sums):
                outs[2][i : i + 1, :] = value


def lead_kernel(*refs, spans, bit, chunk):
    cols, refs = refs[: spans - 1], refs[spans - 1 :]
    rheads, refs = (refs[: spans - 1], refs[spans - 1 :]) if chunk else (cols, refs)
    keep, recv, log, refs = refs[0], refs[1], refs[2], refs[3:]
    head, (mine, send) = (refs[0], refs[1:]) if chunk else (recv, refs)
    rows = keep.shape[0]
    span = lax.axis_index("seq")
    state = jnp.zeros(keep.shape, F32)
    earlier = [span ^ k for k in range(1, spans)]
    decays = [jnp.where(s < span, get_log(ref, chunk), 0.0) for s, ref in zip(earlier, rheads)]
    for s, col in zip(earlier, cols):
        behind = jnp.zeros_like(decays[0])
        for t, decay in zip(earlier, decays):
            behind = behind + jnp.where(t > s, decay, 0.0)
        state = state + jnp.where(s < span, jnp.exp(behind) * col[0:rows, :].astype(F32), 0.0)
    decay = jnp.exp(pair_of(log[chunk : chunk + 1, :], get_log(head, chunk), bit)[0])
    moved = decay * state + pair_of(keep[...], recv[0:rows, :].astype(F32), bit)[0]
    here, there = pair_of(state, moved, bit)
    mine[...] = here
    send[...] = there.astype(BF16)


def down_kernel(*refs, bit, chunk):
    base, rbase, keep, recv, log = refs[:5]
    head = refs[5] if chunk else recv
    mine, send = refs[-2:]
    rows = keep.shape[0]
    size = rows // 2
    decay = jnp.exp(pair_of(log[chunk : chunk + 1, :], get_log(head, chunk), bit)[0])
    for where, source in zip(halves(2 * bit), (base, rbase)):
        here = rows_at(where * size, size)
        state = source[...].astype(F32)
        moved = decay * state + pair_of(keep[here, :], recv[here, :].astype(F32), bit)[0]
        ahead, there = pair_of(state, moved, bit)
        mine[here, :] = ahead
        send[here, :] = there.astype(BF16)


def split_chip_kernel(own, rec, table, rtable, keep, first_out, second_out, *logs_out, chunk, firsts, sizes, half, dkey):
    rows = keep.shape[0]
    base = table.shape[0] - CORES * half
    (kept, sent), (stay, go) = halves(1), halves(2)
    part = rows // 2
    for where, start, size, target in (
        (kept, kept * rows, rows, keep),
        (sent, sent * rows + go * part, part, first_out),
        (sent, sent * rows + stay * part, part, second_out),
    ):
        here = rows_at(start, part) if size == part else rows_at(start, rows)
        heads = [base + first + (where * count) // dkey for first, count in zip(firsts, sizes)]
        logs = [(table[pl.ds(head, 1), :], rtable[pl.ds(head + half, 1), :]) for head in heads]
        decay = jnp.exp(pair_of(*logs[chunk], 1, "core")[1])
        early, late = pair_of(own[here, :], rec[here, :], 1, "core")
        target[0:size, :] = (decay * early + late).astype(target.dtype)
        if chunk == 0 and target is first_out:
            put_logs(target, [x + y for x, y in logs])
        if chunk == 0 and target is keep:
            for i, (x, y) in enumerate(logs):
                logs_out[0][i : i + 1, :] = x + y


def part_up_kernel(keep, recv, log, *refs, chunk, going):
    head, outs = (refs[0], refs[1:]) if chunk or not going else (recv, refs)
    size = keep.shape[0] // 2
    here = rows_at(halves(2)[1 if going else 0] * size, size)
    decay = jnp.exp(pair_of(log[chunk : chunk + 1, :], get_log(head, chunk), 1)[1])
    early, late = pair_of(keep[here, :], recv[0:size, :].astype(F32), 1)
    outs[0][0:size, :] = (decay * early + late).astype(outs[0].dtype)
    if chunk == 0 and going:
        sums = [log[i : i + 1, :] + get_log(head, i) for i in range(CHUNKS)]
        put_logs(outs[0], sums)
        for i, value in enumerate(sums):
            outs[1][i : i + 1, :] = value


def part_down_kernel(base, keep, recv, log, head, mine, send, *, chunk, going):
    size = base.shape[0]
    here = rows_at(halves(2)[1 if going else 0] * size, size)
    decay = jnp.exp(pair_of(log[chunk : chunk + 1, :], get_log(head, chunk), 1)[0])
    state = base[...].astype(F32)
    moved = decay * state + pair_of(keep[here, :], recv[0:size, :].astype(F32), 1)[0]
    ahead, there = pair_of(state, moved, 1)
    mine[...] = ahead
    send[...] = there.astype(BF16)


def spread_kernel(*refs, first, half, dkey):
    parts, (own, rec, table, rtable, mine, other) = refs[:-6], refs[-6:]
    size = parts[0].shape[0]
    start = table.shape[0] - CORES * half
    places = halves(1)
    if len(parts) == 4:
        places = [2 * where + part for where in halves(1) for part in halves(2)]
    for where, source in zip(places, parts):
        here = rows_at(where * size, size)
        head = start + first + (where * size) // dkey
        decay = jnp.exp(pair_of(table[pl.ds(head, 1), :], rtable[pl.ds(head + half, 1), :], 1, "core")[0])
        state = source[...].astype(F32)
        moved = decay * state + pair_of(own[here, :], rec[here, :], 1, "core")[0]
        ahead, there = pair_of(state, moved, 1, "core")
        mine[here, :] = ahead.astype(BF16)
        other[here, :] = there.astype(BF16)


def gate_kernel(og, gain, out, *, half, dval):
    for j in range(CORES * half):
        at = head_cols(j, half, dval)
        out[:, j * dval : (j + 1) * dval] = gain[:, at].astype(F32) * jax.nn.sigmoid(og[:, at].astype(F32))


def intra_kernel(q, k, v, rowa, cols, out, *, half, dkey, dval, scale):
    tok = q.shape[0]
    rows = lax.broadcasted_iota(jnp.int32, (tok, tok), 0)
    lanes = lax.broadcasted_iota(jnp.int32, (tok, tok), 1)
    causal = lanes <= rows
    for j in range(CORES * half):
        at = head_cols(j, half, dkey)
        scores = lax.dot_general(q[:, at], k[:, at], (((1,), (1,)), ((), ())), preferred_element_type=F32)
        logw = jnp.where(causal, cols[:, j : j + 1] + rowa[j : j + 1, :], -jnp.inf)
        prod = (scores / scale * jnp.exp(logw)).astype(BF16)
        out[:, j * dval : (j + 1) * dval] = jnp.dot(
            prod, v[:, head_cols(j, half, dval)], preferred_element_type=F32
        )


def final_body(q, state, intra, cols, gate, first, per, half, put):
    heads = CORES * half
    dkey, dval = state.shape[0] // per, state.shape[1]
    for j in range(per):
        head = first + j
        here = slice(head * dval, (head + 1) * dval)
        inter = jnp.dot(
            q[:, head_cols(head, half, dkey)], state[j * dkey : (j + 1) * dkey, :], preferred_element_type=F32
        )
        decay = cols[:, 2 * heads + head : 2 * heads + head + 1]
        hval = (intra[:, here] + decay * inter).astype(BF16).astype(F32)
        meansq = jnp.mean(hval * hval, axis=1, keepdims=True)
        normed = hval * lax.rsqrt(meansq + 1e-06)
        put(j, (normed * gate[:, here]).astype(BF16))


def final_own_kernel(q, state, intra, cols, gate, out, *, first, per, half):
    dval = state.shape[1]

    def put(j, value):
        out[:, j * dval : (j + 1) * dval] = value

    final_body(q, state, intra, cols, gate, first, per, half, put)


def final_other_kernel(q, state, intra, cols, gate, own, *rest, first, per, half):
    out, block, sems = rest[-3:]
    dval = state.shape[1]
    moves = []

    def move(source, head, j):
        target = out.at[:, head_cols(head, half, dval)]
        moves.append(pltpu.make_async_copy(source.at[:, j * dval : (j + 1) * dval], target, sems.at[len(moves)]))
        moves[-1].start()

    for j in range(per):
        move(own, first - half + j, j)

    def put(j, value):
        block[:, j * dval : (j + 1) * dval] = value
        move(block, first + j, j)

    final_body(q, state, intra, cols, gate, first, per, half, put)
    for copy in moves:
        copy.wait()


def final_other(ins, out, *, first, per, half, dval):
    tok = ins[0].shape[0]
    vmem, hbm = pl.BlockSpec(memory_space=pltpu.VMEM), pl.BlockSpec(memory_space=pltpu.HBM)
    specs = [vmem] * len(ins)
    aliases = {}
    if out is not None:
        aliases = {len(ins): 0}
        ins, specs = ins + [out], specs + [hbm]
    return pl.pallas_call(
        functools.partial(final_other_kernel, first=first, per=per, half=half),
        out_shape=shape((tok, CORES * half * dval), BF16),
        in_specs=specs,
        out_specs=hbm,
        scratch_shapes=[pltpu.VMEM((tok, per * dval), BF16), pltpu.SemaphoreType.DMA((2 * per,))],
        input_output_aliases=aliases,
        compiler_params=pltpu.CompilerParams(vmem_limit_bytes=8 << 20),
    )(*ins)


def shards(qproj, kproj, vproj, igate, fgate, ogate, norm_gain):
    spans, nz = lax.axis_size("seq"), lax.axis_size("z")
    tok, heads = igate.shape
    dkey = qproj.shape[1] // heads
    dval = vproj.shape[1] // heads
    half = heads // CORES
    unit = half // sum(SHARES)
    pers = [unit * share for share in SHARES]
    firsts = [sum(pers[:i]) for i in range(CHUNKS)]
    zbits = [1 << j for j in range(nz.bit_length() - 1)]
    sizes = [[per * dkey >> (j + 1) for j in range(len(zbits))] for per in pers]
    assert min(pers) * dkey % (16 * nz) == 0 and max(pers) <= 2 and PIECES * CHUNKS <= PAD
    assert nz == 2 * zbits[-1] and spans & (spans - 1) == 0
    scale = math.sqrt(dkey)

    def swap(a, axis, bit):
        pairs = [(j, j ^ bit) for j in range(lax.axis_size(axis))]
        return lax.ppermute(a, axis, pairs)

    vmem, hbm = pl.BlockSpec(memory_space=pltpu.VMEM), pl.BlockSpec(memory_space=pltpu.HBM)
    in_hbm = lambda *arrays: [pltpu.with_memory_space_constraint(a, pltpu.HBM) for a in arrays]
    params = pltpu.CompilerParams(vmem_limit_bytes=8 << 20)
    rowa, cols, table = pl.pallas_call(
        functools.partial(first_kernel, scale=scale, first=half, per=pers[0]),
        out_shape=[shape((heads, tok), F32), shape((tok, 3 * heads), F32), shape((pers[0] * dkey + heads, dval), F32)],
        in_specs=[hbm] * 4,
        out_specs=[vmem] * 3,
        scratch_shapes=[
            pltpu.VMEM(kproj.shape, BF16),
            pltpu.VMEM(vproj.shape, BF16),
            pltpu.VMEM((heads, tok), BF16),
            pltpu.VMEM((heads, tok), BF16),
            pltpu.SemaphoreType.DMA((4,)),
        ],
        compiler_params=params,
        name="first",
    )(*in_hbm(igate.T, fgate.T, kproj, vproj))
    stretches = [(firsts[0], pers[0])] + [(half + f, p) for f, p in zip(firsts[1:], pers[1:])]
    projections = [shape(a.shape, BF16) for a in (qproj, kproj, vproj)]
    memory = lambda where: [shape((p * dkey, dval), F32) for _, p in where]
    own, *others = pl.pallas_call(
        functools.partial(early_kernel, stretches=stretches, half=half, dkey=dkey),
        out_shape=memory(stretches),
        in_specs=[hbm] * 2 + [vmem],
        out_specs=[vmem] * len(stretches),
        scratch_shapes=[pltpu.VMEM(a.shape, BF16) for a in projections[1:]]
        + [pltpu.SemaphoreType.DMA((2 * len(stretches),))],
        compiler_params=params,
        name="early",
    )(*in_hbm(kproj, vproj), cols)
    stretches = list(zip(firsts[1:], pers[1:])) + stretches + [(half, pers[0])]
    built = CHUNKS - 1
    *owns, qvm, kvm, vvm = pl.pallas_call(
        functools.partial(rest_kernel, stretches=stretches, built=built, half=half, dkey=dkey),
        out_shape=memory(stretches[:built]) + projections,
        in_specs=[hbm] * 3 + [vmem],
        out_specs=[vmem] * (built + 3),
        scratch_shapes=[pltpu.SemaphoreType.DMA((2 * len(stretches) + 1,))],
        compiler_params=params,
        name="rest",
    )(*in_hbm(qproj, kproj, vproj), cols)
    others, owns = [table] + others, [own] + owns
    recs = [swap(other, "core", 1) for other in others]
    rtable = recs[0]

    pads = [PAD] + [0] * (CHUNKS - 1)
    gate = call(
        functools.partial(gate_kernel, half=half, dval=dval),
        [shape((tok, heads * dval), F32)],
        [ogate, norm_gain.reshape(1, heads * dval)],
    )[0]
    intra = call(
        functools.partial(intra_kernel, half=half, dkey=dkey, dval=dval, scale=scale),
        [shape((tok, heads * dval), F32)],
        [qvm, kvm, vvm, rowa, cols],
    )[0]
    logs_shape = [shape((PAD, dval), F32)]
    if len(zbits) == 2:
        f32, bf16 = lambda n: shape((n, dval), F32), lambda n: shape((n, dval), BF16)
        keeps, recvs, seconds, logs, totals, bases = [], [], [], [], [], []
        for i in range(CHUNKS):
            size = sizes[i][1]
            extra = logs_shape if i == 0 else []
            keep, send, second, *log = call(
                functools.partial(
                    split_chip_kernel, chunk=i, firsts=firsts, sizes=[n[0] for n in sizes], half=half, dkey=dkey
                ),
                [f32(2 * size), bf16(size + pads[i]), bf16(size)] + extra,
                [owns[i], recs[i], table, rtable],
            )
            logs += log
            recvs.append([swap(send, "z", 1)])
            seconds.append(swap(second, "z", 1))
            send, *log = call(
                functools.partial(part_up_kernel, chunk=i, going=True),
                [bf16(size + pads[i])] + extra,
                [keep, recvs[i][0], logs[0]] + ([recvs[0][0]] if i else []),
            )
            logs += log
            recvs[i].append(swap(send, "z", 2))
            stay = call(
                functools.partial(part_up_kernel, chunk=i, going=False),
                [f32(size)],
                [keep, seconds[i], logs[0], recvs[0][0]],
            )[0]
            keeps.append([keep, stay])
            total = call(
                functools.partial(up_kernel, bit=2, chunk=i),
                [bf16(size + pads[i])],
                [keeps[i][1], recvs[i][1], logs[1]] + ([recvs[0][1]] if i else []),
            )[0]
            totals.append([swap(total, "seq", k) for k in range(1, spans)])
            mine, send = call(
                functools.partial(lead_kernel, spans=spans, bit=zbits[-1], chunk=i),
                [shape((sizes[i][-1], dval), F32), shape((sizes[i][-1], dval), BF16)],
                totals[i] + (totals[0] if i else []) + [keeps[i][-1], recvs[i][-1], logs[-1]]
                + ([recvs[0][-1]] if i else []),
            )
            far = swap(send, "z", 2)
            near = []
            for base, recv, going in ((mine, seconds[i], False), (far, recvs[i][0], True)):
                mine, send = call(
                    functools.partial(part_down_kernel, chunk=i, going=going),
                    [f32(size), bf16(size)],
                    [base, keep, recv, logs[0], recvs[0][0]],
                )
                near.append((mine, swap(send, "z", 1)))
            bases.append([near[0][0], near[1][0], near[0][1], near[1][1]])
    else:
        keeps, recvs, logs = [], [], []
        for i in range(CHUNKS):
            keep, send, *log = call(
                functools.partial(
                    chip_kernel, chunk=i, firsts=firsts, sizes=[size[0] for size in sizes], half=half, dkey=dkey
                ),
                [shape((sizes[i][0], dval), F32), shape((sizes[i][0] + pads[i], dval), BF16)] + (logs_shape if i == 0 else []),
                [owns[i], recs[i], table, rtable],
            )
            keeps.append([keep])
            recvs.append([swap(send, "z", 1)])
            logs += log

        totals = []
        for level, bit in enumerate(zbits):
            last = bit == zbits[-1]
            for i in range(CHUNKS):
                size = sizes[i][level]
                if last:
                    outs = [shape((size + pads[i], dval), BF16)]
                else:
                    outs = [shape((size // 2, dval), F32), shape((size // 2 + pads[i], dval), BF16)]
                    outs += logs_shape if i == 0 else []
                keep, *send = call(
                    functools.partial(up_kernel, bit=bit, chunk=i),
                    outs,
                    [keeps[i][level], recvs[i][level], logs[level]] + ([recvs[0][level]] if i else []),
                )
                if last:
                    totals.append([swap(keep, "seq", k) for k in range(1, spans)])
                else:
                    keeps[i].append(keep)
                    recvs[i].append(swap(send[0], "z", 2 * bit))
                    logs += send[1:]

        bases = []
        for i in range(CHUNKS):
            mine, send = call(
                functools.partial(lead_kernel, spans=spans, bit=zbits[-1], chunk=i),
                [shape((sizes[i][-1], dval), F32), shape((sizes[i][-1], dval), BF16)],
                totals[i] + (totals[0] if i else []) + [keeps[i][-1], recvs[i][-1], logs[-1]]
                + ([recvs[0][-1]] if i else []),
            )
            bases.append((mine, swap(send, "z", zbits[-1])))
        for level in range(len(zbits) - 2, -1, -1):
            bit = zbits[level]
            for i in range(CHUNKS):
                mine, send = call(
                    functools.partial(down_kernel, bit=bit, chunk=i),
                    [shape((sizes[i][level], dval), F32), shape((sizes[i][level], dval), BF16)],
                    list(bases[i]) + [keeps[i][level], recvs[i][level], logs[level]] + ([recvs[0][level]] if i else []),
                )
                bases[i] = (mine, swap(send, "z", bit))
    out = None
    for i in range(CHUNKS):
        mine, other = call(
            functools.partial(spread_kernel, first=firsts[i], half=half, dkey=dkey),
            [shape((pers[i] * dkey, dval), BF16)] * 2,
            list(bases[i]) + [owns[i], recs[i], table, rtable],
        )
        back = swap(other, "core", 1)
        own = call(
            functools.partial(final_own_kernel, first=firsts[i], per=pers[i], half=half),
            [shape((tok, pers[i] * dval), BF16)],
            [qvm, mine, intra, cols, gate],
        )[0]
        out = final_other(
            [qvm, back, intra, cols, gate, own], out,
            first=half + firsts[i], per=pers[i], half=half, dval=dval,
        )
    return out


def solution(mesh):
    spans, lanes = mesh.shape["seq"], mesh.shape["hv"]
    nz = lanes // CORES
    inner = Mesh(mesh.devices.reshape(spans, nz, CORES), ("seq", "z", "core"))
    split = P(("seq", "z", "core"), None)

    return jax.shard_map(shards, mesh=inner, in_specs=(split,) * 6 + (P(),), out_specs=split, check_vma=False)
```
